32 devices in a mesh: dp: 16 (over z, y, x), tensor: 2 (over core).
Axes of the slice: x: 2, y: 2, z: 4, core: 2. Of those that a mesh axis runs over, the one named last changes fastest.
Arguments:
- tokens: bfloat16 [4096, 768], P(('dp', 'tensor')), may hold values from -6 to 6
- segments: int32 [4096], P('dp'), may hold values from 0 to 7, as said below
- attention_gain: float32 [768], replicated, may hold values from 0.1 to 1.9
- attention_shift: float32 [768], replicated, may hold values from -3 to 3
- query_key_value: bfloat16 [768, 3, 768], P(None, None, 'tensor'), may hold values from -0.21875 to 0.21875
- query_value_bias: float32 [2, 768], P(None, 'tensor'), may hold values from -3 to 3
- output_weight: bfloat16 [768, 768], P('tensor'), may hold values from -0.875 to 0.875
- output_bias: float32 [768], replicated, may hold values from -3 to 3
- feedforward_gain: float32 [768], replicated, may hold values from 0.1 to 1.9
- feedforward_shift: float32 [768], replicated, may hold values from -3 to 3
- expand_weight: bfloat16 [768, 3072], P(None, 'tensor'), may hold values from -0.21875 to 0.21875
- expand_bias: float32 [3072], P('tensor'), may hold values from -3 to 3
- contract_weight: bfloat16 [3072, 768], P('tensor'), may hold values from -0.21875 to 0.21875
- contract_bias: float32 [768], replicated, may hold values from -3 to 3
- cotangent: bfloat16 [4096, 768], P(('dp', 'tensor')), may hold values from -6 to 6
Outputs:
- block_output: float32 [4096, 768], P(('dp', 'tensor'))
- input_gradient: float32 [4096, 768], P(('dp', 'tensor'))
- attention_gain_gradient: float32 [768], replicated
- attention_shift_gradient: float32 [768], replicated
- query_key_value_gradient: float32 [768, 3, 768], P('dp', None, 'tensor')
- query_value_bias_gradient: float32 [2, 768], P(None, 'tensor')
- output_weight_gradient: float32 [768, 768], P('tensor', 'dp')
- output_bias_gradient: float32 [768], replicated
- feedforward_gain_gradient: float32 [768], replicated
- feedforward_shift_gradient: float32 [768], replicated
- expand_weight_gradient: float32 [768, 3072], P('dp', 'tensor')
- expand_bias_gradient: float32 [3072], P('tensor')
- contract_weight_gradient: float32 [3072, 768], P('tensor', 'dp')
- contract_bias_gradient: float32 [768], replicated
The draws below stay inside these ranges and needn't reach their ends.
Inputs may be any that keep to these rules, and one draw needn't show every extreme that they name: `segments`: within each pack of 256 tokens the numbers start at 0, never fall and rise by at most one from token to token; a sequence is a run of one number in one pack and holds 1 to 256 tokens; some sequence holds exactly 256; some pack holds 8 sequences.
All inputs are finite; a program needn't handle non-finite values.
Results may differ from the reference program's by a relative error of at most 0.012.
The reference program's roundings to bfloat16 on the way (of `normed_one`, `mixed`, `normed_two`, `after`, `d_mixed` and `d_scores`) count: a program that leaves them out, or rounds other values in their place, can miss the bound.
Values may be sent and summed in bfloat16 or wider, within the bound.
A program may use at most 128 MiB of HBM per device.

```python
import jax
import jax.numpy as jnp
from jax import lax

D = 768
FF = 3072
HEAD_DIM = 64
PACK = 256
MAXLEN = 256
SPLITS = 8
TOKENS = 4096


def draw_segments(key, part):
    packs = TOKENS // PACK
    key_count, key_order, key_score = jax.random.split(jax.random.fold_in(key, 11), 3)
    count = jax.random.randint(key_count, (packs,), 1, SPLITS + 1)
    order = jax.random.permutation(key_order, packs)
    count = jnp.where(order == 0, 1, jnp.where(order == 1, SPLITS, count))
    place = jnp.arange(PACK, dtype=jnp.int32)
    forced = (place % MAXLEN == 0) & (place > 0)
    score = jax.random.randint(key_score, (packs, PACK), 0, 1 << 20) * PACK + place[None, :]
    barred = forced[None, :] | (place[None, :] == 0)
    score = jnp.where(barred, (1 << 30) + place[None, :], score)
    rank = jnp.argsort(jnp.argsort(score, axis=1), axis=1)
    chosen = (rank < (count - 1)[:, None]) | forced[None, :]
    numbers = jnp.cumsum(chosen.astype(jnp.int32), axis=1)
    return numbers.reshape(TOKENS).astype(jnp.int32)


def block_scale(key, shape, shards, smallest, largest):
    def one(dim, blocks):
        heights = jax.random.uniform(jax.random.fold_in(jax.random.fold_in(key, 6), dim), (blocks,), jnp.float32, smallest / len(shards), largest / len(shards))
        return jnp.repeat(jnp.exp(heights), shape[dim] // blocks).reshape((-1,) + (1,) * (len(shape) - dim - 1))

    factor_of = one(*shards[0])
    for cut in shards[1:]:
        factor_of = factor_of * one(*cut)
    return factor_of


def bell_draw(own_key, extent, scale, most, cuts=(), kind=jnp.bfloat16):
    factor_of = block_scale(own_key, extent, cuts, -0.22, 0.18) if cuts else 1.0
    values = jax.random.normal(own_key, extent, jnp.float32) * scale * factor_of
    return jnp.minimum(jnp.maximum(values, -most), most).astype(kind)


def setup_inputs(seed: int = 0) -> dict:
    splits = jax.random.split(jax.random.key(seed), 16)
    return {
        "tokens": bell_draw(splits[0], (TOKENS, D), 1.0, 6.0, ((0, 32),)),
        "segments": draw_segments(jax.random.fold_in(splits[15], 71), 0),
        "attention_gain": jnp.clip(1.0 + 0.18 * jax.random.normal(splits[2], (D,), jnp.float32), 0.1, 1.9),
        "attention_shift": bell_draw(splits[3], (D,), 0.5, 3.0, (), jnp.float32),
        "query_key_value": bell_draw(splits[4], (D, 3, D), D ** -0.5, 0.21875, ((2, 2),)),
        "query_value_bias": bell_draw(splits[5], (2, D), 0.5, 3.0, ((1, 2),), jnp.float32),
        "output_weight": bell_draw(splits[6], (D, D), (D // 16) ** -0.5, 0.875, ((0, 2),)),
        "output_bias": bell_draw(splits[7], (D,), 0.5, 3.0, (), jnp.float32),
        "feedforward_gain": jnp.clip(1.0 + 0.18 * jax.random.normal(splits[8], (D,), jnp.float32), 0.1, 1.9),
        "feedforward_shift": bell_draw(splits[9], (D,), 0.5, 3.0, (), jnp.float32),
        "expand_weight": bell_draw(splits[10], (D, FF), D ** -0.5, 0.21875, ((1, 2),)),
        "expand_bias": bell_draw(splits[11], (FF,), 0.5, 3.0, ((0, 2),), jnp.float32),
        "contract_weight": bell_draw(splits[12], (FF, D), (FF // 4) ** -0.5, 0.21875, ((0, 2),)),
        "contract_bias": bell_draw(splits[13], (D,), 0.5, 3.0, (), jnp.float32),
        "cotangent": bell_draw(splits[14], (TOKENS, D), 1.0, 6.0, ((0, 32),)),
    }


epsilon = 1e-05

def normalize(values, gain, shift):
    center = lax.optimization_barrier(jnp.mean(values, axis=-1, keepdims=True))
    centered = values - center
    spread = lax.optimization_barrier(jnp.mean(centered * centered, axis=-1, keepdims=True))
    inverse = lax.rsqrt(spread + epsilon)
    unit = centered * inverse
    return (unit * gain + shift, unit, inverse)

def normalize_back(unit, inverse, gain, incoming):
    scaled = incoming * gain
    first = lax.optimization_barrier(jnp.mean(scaled, axis=-1, keepdims=True))
    second = lax.optimization_barrier(jnp.mean(scaled * unit, axis=-1, keepdims=True))
    return inverse * (scaled - first - unit * second)

def gelu_tanh(values):
    return jax.nn.gelu(values, approximate=True)

def allowed_pairs(segments):
    count = segments.shape[0]
    query_place = lax.broadcasted_iota(jnp.int32, (count, count), 0)
    key_place = lax.broadcasted_iota(jnp.int32, (count, count), 1)
    return (key_place <= query_place) & (segments[:, None] == segments[None, :])

def one_pack(tokens, segments, cotangent, attention_gain, attention_shift, query_key_value, query_value_bias, output_weight, output_bias, feedforward_gain, feedforward_shift, expand_weight, expand_bias, contract_weight, contract_bias):
    length = tokens.shape[0]
    heads_all = D // HEAD_DIM
    scale = HEAD_DIM ** (-0.5)
    flat_weight = query_key_value.reshape(D, 3 * D)
    residual_in = tokens.astype(jnp.float32)
    normed_one, unit_one, inverse_one = normalize(residual_in, attention_gain, attention_shift)
    normed_one = normed_one.astype(jnp.bfloat16)
    joined = jnp.dot(normed_one, flat_weight, preferred_element_type=jnp.float32).reshape(length, 3, D)
    query = (joined[:, 0] + query_value_bias[0]).astype(jnp.bfloat16).reshape(length, heads_all, HEAD_DIM)
    keys = joined[:, 1].astype(jnp.bfloat16).reshape(length, heads_all, HEAD_DIM)
    values = (joined[:, 2] + query_value_bias[1]).astype(jnp.bfloat16).reshape(length, heads_all, HEAD_DIM)
    allowed = allowed_pairs(segments)[None]
    scores = jnp.einsum('qhe,khe->hqk', query.astype(jnp.float32), keys.astype(jnp.float32)) * scale
    masked = jnp.where(allowed, scores, -1e+30)
    highest = lax.optimization_barrier(jnp.max(masked, axis=2, keepdims=True))
    log_total = highest + jnp.log(lax.optimization_barrier(jnp.sum(jnp.exp(masked - highest), axis=2, keepdims=True)))
    weights = jnp.where(allowed, jnp.exp(masked - log_total), 0.0)
    weights_low = weights.astype(jnp.bfloat16)
    mixed = jnp.einsum('hqk,khe->qhe', weights_low.astype(jnp.float32), values.astype(jnp.float32))
    mixed = mixed.astype(jnp.bfloat16)
    mixed_flat = mixed.reshape(length, D)
    hidden = residual_in + jnp.dot(mixed_flat, output_weight, preferred_element_type=jnp.float32) + output_bias
    normed_two, unit_two, inverse_two = normalize(hidden, feedforward_gain, feedforward_shift)
    normed_two = normed_two.astype(jnp.bfloat16)
    before = jnp.dot(normed_two, expand_weight, preferred_element_type=jnp.float32) + expand_bias
    after, gelu_back = jax.vjp(gelu_tanh, before)
    after_low = after.astype(jnp.bfloat16)
    block_output = hidden + jnp.dot(after_low, contract_weight, preferred_element_type=jnp.float32) + contract_bias
    upstream = cotangent.astype(jnp.float32)
    contract_bias_grad = lax.optimization_barrier(jnp.sum(upstream, axis=0))
    contract_grad = jnp.dot(after_low.T, cotangent, preferred_element_type=jnp.float32)
    d_after = jnp.dot(cotangent, contract_weight.T, preferred_element_type=jnp.float32)
    d_before = gelu_back(d_after)[0]
    expand_bias_grad = lax.optimization_barrier(jnp.sum(d_before, axis=0))
    d_before_low = d_before.astype(jnp.bfloat16)
    expand_grad = jnp.dot(normed_two.T, d_before_low, preferred_element_type=jnp.float32)
    d_normed_two = jnp.dot(d_before_low, expand_weight.T, preferred_element_type=jnp.float32)
    feed_gain_grad = lax.optimization_barrier(jnp.sum(d_normed_two * unit_two, axis=0))
    feed_shift_grad = lax.optimization_barrier(jnp.sum(d_normed_two, axis=0))
    d_hidden = upstream + normalize_back(unit_two, inverse_two, feedforward_gain, d_normed_two)
    output_bias_grad = lax.optimization_barrier(jnp.sum(d_hidden, axis=0))
    d_hidden_low = d_hidden.astype(jnp.bfloat16)
    output_grad = jnp.dot(mixed_flat.T, d_hidden_low, preferred_element_type=jnp.float32)
    d_mixed = jnp.dot(d_hidden_low, output_weight.T, preferred_element_type=jnp.float32).astype(jnp.bfloat16)
    d_mixed = d_mixed.reshape(length, heads_all, HEAD_DIM)
    d_weights = jnp.einsum('qhe,khe->hqk', d_mixed.astype(jnp.float32), values.astype(jnp.float32))
    delta = lax.optimization_barrier(jnp.sum(d_mixed.astype(jnp.float32) * mixed.astype(jnp.float32), axis=2)).T
    d_scores = (weights * (d_weights - delta[:, :, None]) * scale).astype(jnp.bfloat16)
    d_values = jnp.einsum('hqk,qhe->khe', weights_low.astype(jnp.float32), d_mixed.astype(jnp.float32))
    d_query = jnp.einsum('hqk,khe->qhe', d_scores.astype(jnp.float32), keys.astype(jnp.float32))
    d_keys = jnp.einsum('hqk,qhe->khe', d_scores.astype(jnp.float32), query.astype(jnp.float32))
    d_query = d_query.reshape(length, D)
    d_keys = d_keys.reshape(length, D)
    d_values = d_values.reshape(length, D)
    bias_grad = jnp.stack([lax.optimization_barrier(jnp.sum(d_query, axis=0)), lax.optimization_barrier(jnp.sum(d_values, axis=0))])
    d_joined_low = jnp.stack([d_query, d_keys, d_values], axis=1).astype(jnp.bfloat16).reshape(length, 3 * D)
    joined_grad = jnp.dot(normed_one.T, d_joined_low, preferred_element_type=jnp.float32).reshape(D, 3, D)
    d_normed_one = jnp.dot(d_joined_low, flat_weight.T, preferred_element_type=jnp.float32)
    first_gain_grad = lax.optimization_barrier(jnp.sum(d_normed_one * unit_one, axis=0))
    first_shift_grad = lax.optimization_barrier(jnp.sum(d_normed_one, axis=0))
    input_gradient = d_hidden + normalize_back(unit_one, inverse_one, attention_gain, d_normed_one)
    gradients = (first_gain_grad, first_shift_grad, joined_grad, bias_grad, output_grad, output_bias_grad, feed_gain_grad, feed_shift_grad, expand_grad, expand_bias_grad, contract_grad, contract_bias_grad)
    return (block_output, input_gradient, gradients)

def reference(tokens, segments, attention_gain, attention_shift, query_key_value, query_value_bias, output_weight, output_bias, feedforward_gain, feedforward_shift, expand_weight, expand_bias, contract_weight, contract_bias, cotangent):
    packs = tokens.shape[0] // PACK
    initial = (jnp.zeros((D,), jnp.float32), jnp.zeros((D,), jnp.float32), jnp.zeros((D, 3, D), jnp.float32), jnp.zeros((2, D), jnp.float32), jnp.zeros((D, D), jnp.float32), jnp.zeros((D,), jnp.float32), jnp.zeros((D,), jnp.float32), jnp.zeros((D,), jnp.float32), jnp.zeros((D, FF), jnp.float32), jnp.zeros((FF,), jnp.float32), jnp.zeros((FF, D), jnp.float32), jnp.zeros((D,), jnp.float32))

    def advance(totals, pieces):
        pack_tokens, pack_segments, pack_cotangent = pieces
        block_output, input_gradient, gradients = one_pack(pack_tokens, pack_segments, pack_cotangent, attention_gain, attention_shift, query_key_value, query_value_bias, output_weight, output_bias, feedforward_gain, feedforward_shift, expand_weight, expand_bias, contract_weight, contract_bias)
        totals = jax.tree.map(lambda left, right: left + right, totals, gradients)
        return (totals, (block_output, input_gradient))
    totals, outputs = lax.scan(advance, initial, (tokens.reshape(packs, PACK, D), segments.reshape(packs, PACK), cotangent.reshape(packs, PACK, D)))
    block_output = outputs[0].reshape(packs * PACK, D)
    input_gradient = outputs[1].reshape(packs * PACK, D)
    return (block_output, input_gradient, totals[0], totals[1], totals[2], totals[3], totals[4], totals[5], totals[6], totals[7], totals[8], totals[9], totals[10], totals[11])
```

```python
import jax
import jax.numpy as jnp
from jax import lax
from jax.sharding import PartitionSpec as P

HEAD_DIM = 64


epsilon = 1e-05


def normalize(values, gain, shift):
    center = jnp.mean(values, axis=-1, keepdims=True)
    centered = values - center
    spread = jnp.mean(centered * centered, axis=-1, keepdims=True)
    inverse = lax.rsqrt(spread + epsilon)
    unit = centered * inverse
    return (unit * gain + shift, unit, inverse)


def normalize_back(unit, inverse, gain, incoming):
    scaled = incoming * gain
    first = jnp.mean(scaled, axis=-1, keepdims=True)
    second = jnp.mean(scaled * unit, axis=-1, keepdims=True)
    return inverse * (scaled - first - unit * second)


def gelu_tanh(values):
    return jax.nn.gelu(values, approximate=True)


def allowed_pairs(segments):
    count = segments.shape[0]
    query_place = lax.broadcasted_iota(jnp.int32, (count, count), 0)
    key_place = lax.broadcasted_iota(jnp.int32, (count, count), 1)
    return (key_place <= query_place) & (segments[:, None] == segments[None, :])


def contract_rows(left, right):
    return lax.dot_general(
        left, right, (((0,), (0,)), ((), ())), preferred_element_type=jnp.float32
    )


def contract_columns(left, right):
    return lax.dot_general(
        left, right, (((1,), (1,)), ((), ())), preferred_element_type=jnp.float32
    )


def attention_weights(query, keys, allowed, scale, log_total):
    scores = jnp.einsum("qhe,khe->hqk", query, keys, preferred_element_type=jnp.float32) * scale
    masked = jnp.where(allowed, scores, -1e30)
    return jnp.where(allowed, jnp.exp(masked - log_total), 0.0)


def select_bit(stack, axis, bit):
    return lax.dynamic_index_in_dim(stack, bit, axis, keepdims=False)


def flip_dp(values, mask):
    count = lax.axis_size("dp")
    return lax.ppermute(values, "dp", [(i, i ^ mask) for i in range(count)])


def swap_tensor(values):
    return lax.ppermute(values, "tensor", [(0, 1), (1, 0)])


def dp_bit(bit):
    return (lax.axis_index("dp") >> bit) & 1


def pick(stack, bits, group, flips):
    left = list(bits)
    for bit in group:
        axis = left.index(bit)
        mine = dp_bit(bit)
        stack = select_bit(stack, axis, 1 - mine if (flips >> bit) & 1 else mine)
        left.remove(bit)
    return stack, left


def masks_of(group):
    masks = [0]
    for bit in group:
        masks = masks + [m | (1 << bit) for m in masks]
    return masks[1:]


def tail_groups(bits):
    rising = sorted(bits)
    return [rising[i : i + 2] for i in range(0, len(rising), 2)]


def scatter_rows(left, right, first, second):
    count = lax.axis_size("dp")
    depth = count.bit_length() - 1
    rows = left.shape[1]
    chunk = rows // count
    bits = list(range(depth - 1, -1, -1))
    turned = left.T.reshape((2,) * depth + (chunk, left.shape[0]))

    def product(flips):
        part, rest = pick(turned, bits, [first], flips)
        block = part.reshape(rows // 2, left.shape[0])
        return jnp.dot(block, right, preferred_element_type=jnp.float32), rest

    outgoing, rest = product(1 << first)
    arrived = flip_dp(outgoing.astype(jnp.bfloat16), 1 << first)
    total = product(0)[0] + arrived.astype(jnp.float32)
    total = total.reshape((2,) * (depth - 1) + (chunk, right.shape[1]))
    groups = [[second]] + tail_groups([b for b in rest if b != second])
    for group in groups:
        arrivals = []
        for mask in masks_of(group):
            piece = pick(total, rest, group, mask)[0].astype(jnp.bfloat16)
            arrivals.append(flip_dp(piece, mask))
        total, rest = pick(total, rest, group, 0)
        for piece in arrivals:
            total = total + piece.astype(jnp.float32)
    return total


def sum_dp(values):
    depth = lax.axis_size("dp").bit_length() - 1
    for group in [[0], [1]] + tail_groups(range(2, depth)):
        parts = [values] + [flip_dp(values, mask) for mask in masks_of(group)]
        while len(parts) > 1:
            parts = [parts[i] + parts[i + 1] for i in range(0, len(parts), 2)]
        values = parts[0]
    return values


def scatter_tensor(partial):
    half = partial.shape[0] // 2
    core = lax.axis_index("tensor")
    away = lax.dynamic_slice_in_dim(partial, (1 - core) * half, half, 0)
    mine = lax.dynamic_slice_in_dim(partial, core * half, half, 0)
    return mine + swap_tensor(away)


def shards(
    tokens,
    segments,
    attention_gain,
    attention_shift,
    query_key_value,
    query_value_bias,
    output_weight,
    output_bias,
    feedforward_gain,
    feedforward_shift,
    expand_weight,
    expand_bias,
    contract_weight,
    contract_bias,
    cotangent,
):
    width = tokens.shape[1]
    local = query_key_value.shape[2]
    heads_here = local // HEAD_DIM
    scale = HEAD_DIM ** (-0.5)
    flat_weight = query_key_value.reshape(width, 3 * local)
    residual_in = tokens.astype(jnp.float32)
    normed_share, unit_one, inverse_one = normalize(residual_in, attention_gain, attention_shift)
    normed_share = normed_share.astype(jnp.bfloat16)
    normed_one, cotangent_rows = (
        lax.all_gather(normed_share, "tensor", axis=0, tiled=True),
        lax.all_gather(cotangent, "tensor", axis=0, tiled=True),
    )
    length = normed_one.shape[0]
    joined = jnp.dot(normed_one, flat_weight, preferred_element_type=jnp.float32).reshape(
        length, 3, local
    )
    query = (
        (joined[:, 0] + query_value_bias[0])
        .astype(jnp.bfloat16)
        .reshape(length, heads_here, HEAD_DIM)
    )
    keys = joined[:, 1].astype(jnp.bfloat16).reshape(length, heads_here, HEAD_DIM)
    values = (
        (joined[:, 2] + query_value_bias[1])
        .astype(jnp.bfloat16)
        .reshape(length, heads_here, HEAD_DIM)
    )
    allowed = allowed_pairs(segments)[None]
    scores = jnp.einsum("qhe,khe->hqk", query, keys, preferred_element_type=jnp.float32) * scale
    masked = jnp.where(allowed, scores, -1e30)
    highest = jnp.max(masked, axis=2, keepdims=True)
    log_total = highest + jnp.log(jnp.sum(jnp.exp(masked - highest), axis=2, keepdims=True))
    weights_low = jnp.where(allowed, jnp.exp(masked - log_total), 0.0).astype(jnp.bfloat16)
    mixed = jnp.einsum("hqk,khe->qhe", weights_low, values, preferred_element_type=jnp.float32)
    mixed = mixed.astype(jnp.bfloat16)
    mixed_flat = mixed.reshape(length, local)
    partial_attention = jnp.dot(mixed_flat, output_weight, preferred_element_type=jnp.float32)
    attention_share = scatter_tensor(partial_attention)
    hidden = residual_in + attention_share + output_bias
    normed_two_share, unit_two, inverse_two = normalize(hidden, feedforward_gain, feedforward_shift)
    normed_two = lax.all_gather(normed_two_share.astype(jnp.bfloat16), "tensor", axis=0, tiled=True)
    before = jnp.dot(normed_two, expand_weight, preferred_element_type=jnp.float32) + expand_bias
    after, gelu_back = jax.vjp(gelu_tanh, before)
    after_low = after.astype(jnp.bfloat16)
    partial_feed = jnp.dot(after_low, contract_weight, preferred_element_type=jnp.float32)
    block_output = (
        hidden
        + scatter_tensor(partial_feed)
        + contract_bias
    )
    upstream = cotangent.astype(jnp.float32)
    contract_bias_grad = jnp.sum(upstream, axis=0)
    contract_share = scatter_rows(cotangent_rows, after_low, 0, 1).T
    d_after = contract_columns(cotangent_rows, contract_weight)
    d_before = gelu_back(d_after)[0]
    expand_bias_grad = jnp.sum(d_before, axis=0)
    d_before_low = d_before.astype(jnp.bfloat16)
    expand_share = scatter_rows(normed_two, d_before_low, 1, 0)
    partial_second = contract_columns(d_before_low, expand_weight)
    d_normed_two = scatter_tensor(partial_second)
    feed_gain_grad = jnp.sum(d_normed_two * unit_two, axis=0)
    feed_shift_grad = jnp.sum(d_normed_two, axis=0)
    d_hidden = upstream + normalize_back(unit_two, inverse_two, feedforward_gain, d_normed_two)
    output_bias_grad = jnp.sum(d_hidden, axis=0)
    d_hidden_low = lax.all_gather(d_hidden.astype(jnp.bfloat16), "tensor", axis=0, tiled=True)
    output_share = scatter_rows(d_hidden_low, mixed_flat, 1, 0).T
    early = jnp.stack([output_bias_grad, feed_gain_grad, feed_shift_grad, contract_bias_grad])
    early = early + swap_tensor(early)
    early = sum_dp(jnp.concatenate([early.reshape(-1), expand_bias_grad]))
    d_mixed = contract_columns(d_hidden_low, output_weight).astype(jnp.bfloat16)
    d_mixed = d_mixed.reshape(length, heads_here, HEAD_DIM)
    weights = attention_weights(query, keys, allowed, scale, log_total)
    weights_again = weights.astype(jnp.bfloat16)
    d_weights = jnp.einsum("qhe,khe->hqk", d_mixed, values, preferred_element_type=jnp.float32)
    delta = jnp.einsum("qhe,qhe->hq", d_mixed, mixed, preferred_element_type=jnp.float32)
    d_scores = (weights * (d_weights - delta[:, :, None]) * scale).astype(jnp.bfloat16)
    d_values = jnp.einsum(
        "hqk,qhe->khe", weights_again, d_mixed, preferred_element_type=jnp.float32
    )
    d_query = jnp.einsum("hqk,khe->qhe", d_scores, keys, preferred_element_type=jnp.float32)
    d_keys = jnp.einsum("hqk,qhe->khe", d_scores, query, preferred_element_type=jnp.float32)
    d_query = d_query.reshape(length, local)
    d_keys = d_keys.reshape(length, local)
    d_values = d_values.reshape(length, local)
    bias_grad = jnp.stack([jnp.sum(d_query, axis=0), jnp.sum(d_values, axis=0)])
    d_joined_low = (
        jnp.stack([d_query, d_keys, d_values], axis=1)
        .astype(jnp.bfloat16)
        .reshape(length, 3 * local)
    )
    value_share = scatter_rows(normed_one, d_joined_low[:, 2 * local :], 1, 0)
    other_share = scatter_rows(normed_one, d_joined_low[:, : 2 * local], 0, 1)
    joined_share = jnp.concatenate([other_share, value_share], axis=1).reshape(-1, 3, local)
    partial_first = contract_columns(d_joined_low, flat_weight)
    d_normed_one = scatter_tensor(partial_first)
    first_gain_grad = jnp.sum(d_normed_one * unit_one, axis=0)
    first_shift_grad = jnp.sum(d_normed_one, axis=0)
    input_gradient = d_hidden + normalize_back(unit_one, inverse_one, attention_gain, d_normed_one)
    late = jnp.stack([first_gain_grad, first_shift_grad])
    late = late + swap_tensor(late)
    late = sum_dp(jnp.concatenate([late.reshape(-1), bias_grad.reshape(-1)]))
    late_rows = late[: 2 * width].reshape(2, width)
    early_rows = early[: 4 * width].reshape(4, width)
    return (
        block_output,
        input_gradient,
        late_rows[0],
        late_rows[1],
        joined_share,
        late[2 * width :].reshape(2, local),
        output_share,
        early_rows[0],
        early_rows[1],
        early_rows[2],
        expand_share,
        early[4 * width :],
        contract_share,
        early_rows[3],
    )


def solution(mesh):
    in_specs = (
        P(("dp", "tensor"), None),
        P("dp"),
        P(),
        P(),
        P(None, None, "tensor"),
        P(None, "tensor"),
        P("tensor", None),
        P(),
        P(),
        P(),
        P(None, "tensor"),
        P("tensor"),
        P("tensor", None),
        P(),
        P(("dp", "tensor"), None),
    )
    out_specs = (
        P(("dp", "tensor"), None),
        P(("dp", "tensor"), None),
        P(),
        P(),
        P("dp", None, "tensor"),
        P(None, "tensor"),
        P("tensor", "dp"),
        P(),
        P(),
        P(),
        P("dp", "tensor"),
        P("tensor"),
        P("tensor", "dp"),
        P(),
    )
    return jax.shard_map(shards, mesh=mesh, in_specs=in_specs, out_specs=out_specs, check_vma=False)
```

```python
import jax
import jax.numpy as jnp
from jax import lax
from jax.sharding import PartitionSpec as P

HEAD_DIM = 64


epsilon = 1e-05


def normalize(values, gain, shift):
    center = jnp.mean(values, axis=-1, keepdims=True)
    centered = values - center
    spread = jnp.mean(centered * centered, axis=-1, keepdims=True)
    inverse = lax.rsqrt(spread + epsilon)
    unit = centered * inverse
    return (unit * gain + shift, unit, inverse)


def normalize_back(unit, inverse, gain, incoming):
    scaled = incoming * gain
    first = jnp.mean(scaled, axis=-1, keepdims=True)
    second = jnp.mean(scaled * unit, axis=-1, keepdims=True)
    return inverse * (scaled - first - unit * second)


def gelu_tanh(values):
    return jax.nn.gelu(values, approximate=True)


def allowed_pairs(segments):
    count = segments.shape[0]
    query_place = lax.broadcasted_iota(jnp.int32, (count, count), 0)
    key_place = lax.broadcasted_iota(jnp.int32, (count, count), 1)
    return (key_place <= query_place) & (segments[:, None] == segments[None, :])


def contract_rows(left, right):
    return lax.dot_general(
        left, right, (((0,), (0,)), ((), ())), preferred_element_type=jnp.float32
    )


def contract_columns(left, right):
    return lax.dot_general(
        left, right, (((1,), (1,)), ((), ())), preferred_element_type=jnp.float32
    )


def attention_weights(query, keys, allowed, scale, log_total):
    scores = jnp.einsum("qhe,khe->hqk", query, keys, preferred_element_type=jnp.float32) * scale
    masked = jnp.where(allowed, scores, -1e30)
    return jnp.where(allowed, jnp.exp(masked - log_total), 0.0)


def select_bit(stack, axis, bit):
    return lax.dynamic_index_in_dim(stack, bit, axis, keepdims=False)


def flip_dp(values, mask):
    count = lax.axis_size("dp")
    return lax.ppermute(values, "dp", [(i, i ^ mask) for i in range(count)])


def swap_tensor(values):
    return lax.ppermute(values, "tensor", [(0, 1), (1, 0)])


def dp_bit(bit):
    return (lax.axis_index("dp") >> bit) & 1


def pick(stack, bits, group, flips):
    left = list(bits)
    for bit in group:
        axis = left.index(bit)
        mine = dp_bit(bit)
        stack = select_bit(stack, axis, 1 - mine if (flips >> bit) & 1 else mine)
        left.remove(bit)
    return stack, left


def masks_of(group):
    masks = [0]
    for bit in group:
        masks = masks + [m | (1 << bit) for m in masks]
    return masks[1:]


def tail_groups(bits):
    rising = sorted(bits)
    return [rising[i : i + 2] for i in range(0, len(rising), 2)]


def arrange(left, bit):
    count = lax.axis_size("dp")
    rows = left.shape[1]
    turned = left.T.reshape(count >> (bit + 1), 2, 1 << bit, rows // count, left.shape[0])
    turned = jnp.moveaxis(turned, 1, 0)
    turned = jnp.where(dp_bit(bit) == 1, turned, turned[::-1])
    return turned.reshape(2, rows // 2, left.shape[0])


def product(left, right):
    return jnp.dot(left, right, preferred_element_type=jnp.float32)


def joined_products(pairs, half):
    parts = [product(left[half], right) for left, right in pairs]
    return parts[0] if len(parts) == 1 else jnp.concatenate(parts, axis=1)


def first_outgoing(pairs):
    return joined_products(pairs, 0).astype(jnp.bfloat16)


def first_total(own, arrived):
    total = own + arrived.astype(jnp.float32)
    depth = lax.axis_size("dp").bit_length() - 1
    chunk = total.shape[0] >> (depth - 1)
    return total.reshape((2,) * (depth - 1) + (chunk, total.shape[1]))


def bits_left(*used):
    depth = lax.axis_size("dp").bit_length() - 1
    return [b for b in range(depth - 1, -1, -1) if b not in used]


def send_pieces(total, bits, group):
    return [
        flip_dp(pick(total, bits, group, mask)[0].astype(jnp.bfloat16), mask)
        for mask in masks_of(group)
    ]


def add_pieces(total, bits, group, arrivals):
    total, rest = pick(total, bits, group, 0)
    for piece in arrivals:
        total = total + piece.astype(jnp.float32)
    return total, rest


def cut_pieces(total, bits, group):
    return [pick(total, bits, group, mask)[0].astype(jnp.bfloat16) for mask in masks_of(group)]


def last_steps(total, pieces):
    bits = bits_left(0, 1)
    for group in tail_groups(bits):
        if pieces is None:
            pieces = cut_pieces(total, bits, group)
        arrivals = [flip_dp(piece, mask) for piece, mask in zip(pieces, masks_of(group))]
        total, bits = add_pieces(total, bits, group, arrivals)
        pieces = None
    return total


def sum_dp(values, groups):
    for group in groups:
        parts = [values] + [flip_dp(values, mask) for mask in masks_of(group)]
        while len(parts) > 1:
            parts = [parts[i] + parts[i + 1] for i in range(0, len(parts), 2)]
        values = parts[0]
    return values


def scatter_tensor(partial):
    half = partial.shape[0] // 2
    core = lax.axis_index("tensor")
    away = lax.dynamic_slice_in_dim(partial, (1 - core) * half, half, 0)
    mine = lax.dynamic_slice_in_dim(partial, core * half, half, 0)
    return mine + swap_tensor(away)


def shards(
    tokens,
    segments,
    attention_gain,
    attention_shift,
    query_key_value,
    query_value_bias,
    output_weight,
    output_bias,
    feedforward_gain,
    feedforward_shift,
    expand_weight,
    expand_bias,
    contract_weight,
    contract_bias,
    cotangent,
):
    width = tokens.shape[1]
    local = query_key_value.shape[2]
    heads_here = local // HEAD_DIM
    scale = HEAD_DIM ** (-0.5)
    flat_weight = query_key_value.reshape(width, 3 * local)
    residual_in = tokens.astype(jnp.float32)
    normed_share, unit_one, inverse_one = normalize(residual_in, attention_gain, attention_shift)
    normed_share = normed_share.astype(jnp.bfloat16)
    normed_one, cotangent_rows = (
        lax.all_gather(normed_share, "tensor", axis=0, tiled=True),
        lax.all_gather(cotangent, "tensor", axis=0, tiled=True),
    )
    length = normed_one.shape[0]
    joined = jnp.dot(normed_one, flat_weight, preferred_element_type=jnp.float32).reshape(
        length, 3, local
    )
    query = (
        (joined[:, 0] + query_value_bias[0])
        .astype(jnp.bfloat16)
        .reshape(length, heads_here, HEAD_DIM)
    )
    keys = joined[:, 1].astype(jnp.bfloat16).reshape(length, heads_here, HEAD_DIM)
    values = (
        (joined[:, 2] + query_value_bias[1])
        .astype(jnp.bfloat16)
        .reshape(length, heads_here, HEAD_DIM)
    )
    allowed = allowed_pairs(segments)[None]
    scores = jnp.einsum("qhe,khe->hqk", query, keys, preferred_element_type=jnp.float32) * scale
    masked = jnp.where(allowed, scores, -1e30)
    highest = jnp.max(masked, axis=2, keepdims=True)
    log_total = highest + jnp.log(jnp.sum(jnp.exp(masked - highest), axis=2, keepdims=True))
    weights_low = jnp.where(allowed, jnp.exp(masked - log_total), 0.0).astype(jnp.bfloat16)
    mixed = jnp.einsum("hqk,khe->qhe", weights_low, values, preferred_element_type=jnp.float32)
    mixed = mixed.astype(jnp.bfloat16)
    mixed_flat = mixed.reshape(length, local)
    partial_attention = jnp.dot(mixed_flat, output_weight, preferred_element_type=jnp.float32)
    attention_share = scatter_tensor(partial_attention)
    hidden = residual_in + attention_share + output_bias
    normed_two_share, unit_two, inverse_two = normalize(hidden, feedforward_gain, feedforward_shift)
    normed_two = lax.all_gather(normed_two_share.astype(jnp.bfloat16), "tensor", axis=0, tiled=True)
    before = jnp.dot(normed_two, expand_weight, preferred_element_type=jnp.float32) + expand_bias
    after, gelu_back = jax.vjp(gelu_tanh, before)
    after_low = after.astype(jnp.bfloat16)
    partial_feed = jnp.dot(after_low, contract_weight, preferred_element_type=jnp.float32)
    block_output = (
        hidden
        + scatter_tensor(partial_feed)
        + contract_bias
    )
    upstream = cotangent.astype(jnp.float32)
    contract_bias_grad = jnp.sum(upstream, axis=0)
    contract_pairs = [(arrange(cotangent_rows, 0), after_low)]
    contract_arrived = flip_dp(first_outgoing(contract_pairs), 1)
    d_after = contract_columns(cotangent_rows, contract_weight)
    d_before = gelu_back(d_after)[0]
    expand_bias_grad = jnp.sum(d_before, axis=0)
    d_before_low = d_before.astype(jnp.bfloat16)
    expand_pairs = [(arrange(normed_two, 1), d_before_low)]
    expand_arrived = flip_dp(first_outgoing(expand_pairs), 2)
    partial_second = contract_columns(d_before_low, expand_weight)
    d_normed_two = scatter_tensor(partial_second)
    feed_gain_grad = jnp.sum(d_normed_two * unit_two, axis=0)
    feed_shift_grad = jnp.sum(d_normed_two, axis=0)
    d_hidden = upstream + normalize_back(unit_two, inverse_two, feedforward_gain, d_normed_two)
    output_bias_grad = jnp.sum(d_hidden, axis=0)
    d_hidden_low = lax.all_gather(d_hidden.astype(jnp.bfloat16), "tensor", axis=0, tiled=True)
    d_mixed = contract_columns(d_hidden_low, output_weight).astype(jnp.bfloat16)
    d_mixed = d_mixed.reshape(length, heads_here, HEAD_DIM)
    weights = attention_weights(query, keys, allowed, scale, log_total)
    weights_again = weights.astype(jnp.bfloat16)
    d_weights = jnp.einsum("qhe,khe->hqk", d_mixed, values, preferred_element_type=jnp.float32)
    delta = jnp.einsum("qhe,qhe->hq", d_mixed, mixed, preferred_element_type=jnp.float32)
    d_scores = (weights * (d_weights - delta[:, :, None]) * scale).astype(jnp.bfloat16)
    d_values = jnp.einsum(
        "hqk,qhe->khe", weights_again, d_mixed, preferred_element_type=jnp.float32
    )
    d_query = jnp.einsum("hqk,khe->qhe", d_scores, keys, preferred_element_type=jnp.float32)
    d_keys = jnp.einsum("hqk,qhe->khe", d_scores, query, preferred_element_type=jnp.float32)
    d_query = d_query.reshape(length, local)
    d_keys = d_keys.reshape(length, local)
    d_values = d_values.reshape(length, local)
    bias_grad = jnp.stack([jnp.sum(d_query, axis=0), jnp.sum(d_values, axis=0)])
    d_joined_low = (
        jnp.stack([d_query, d_keys, d_values], axis=1)
        .astype(jnp.bfloat16)
        .reshape(length, 3 * local)
    )
    other_pairs = [(arrange(normed_one, 0), d_joined_low[:, : 2 * local])]
    value_pairs = [
        (arrange(normed_one, 1), d_joined_low[:, 2 * local :]),
        (arrange(d_hidden_low, 1), mixed_flat),
    ]
    other_out = first_outgoing(other_pairs)
    value_out = first_outgoing(value_pairs)
    other_own = joined_products(other_pairs, 1)
    value_own = joined_products(value_pairs, 1)
    partial_first = contract_columns(d_joined_low, flat_weight)
    d_normed_one = scatter_tensor(partial_first)
    (
        d_normed_one,
        other_out,
        value_out,
        other_own,
        value_own,
        contract_arrived,
        expand_arrived,
    ) = lax.optimization_barrier(
        (
            d_normed_one,
            other_out,
            value_out,
            other_own,
            value_own,
            contract_arrived,
            expand_arrived,
        )
    )
    contract_total = first_total(joined_products(contract_pairs, 1), contract_arrived)
    expand_total = first_total(joined_products(expand_pairs, 1), expand_arrived)
    contract_piece = cut_pieces(contract_total, bits_left(0), [1])[0]
    expand_piece = cut_pieces(expand_total, bits_left(1), [0])[0]
    contract_piece, expand_piece, other_out, value_out = lax.optimization_barrier(
        (contract_piece, expand_piece, other_out, value_out)
    )
    contract_arrived = flip_dp(contract_piece, 2)
    expand_arrived = flip_dp(expand_piece, 1)
    other_arrived = flip_dp(other_out, 1)
    value_arrived = flip_dp(value_out, 2)
    first_gain_grad = jnp.sum(d_normed_one * unit_one, axis=0)
    first_shift_grad = jnp.sum(d_normed_one, axis=0)
    input_gradient = d_hidden + normalize_back(unit_one, inverse_one, attention_gain, d_normed_one)
    rows = jnp.concatenate(
        [
            first_gain_grad,
            first_shift_grad,
            output_bias_grad,
            feed_gain_grad,
            feed_shift_grad,
            contract_bias_grad,
        ]
    )
    rows = rows + swap_tensor(rows)
    depth = lax.axis_size("dp").bit_length() - 1
    sums = sum_dp(
        jnp.concatenate([rows, bias_grad.reshape(-1), expand_bias_grad]),
        tail_groups(range(2, depth)),
    )
    sums, contract_arrived, expand_arrived = lax.optimization_barrier(
        (sums, contract_arrived, expand_arrived)
    )
    contract_total = add_pieces(contract_total, bits_left(0), [1], [contract_arrived])[0]
    expand_total = add_pieces(expand_total, bits_left(1), [0], [expand_arrived])[0]
    feed_total = jnp.concatenate([contract_total, expand_total], axis=-1)
    bits = bits_left(0, 1)
    pieces = cut_pieces(feed_total, bits, tail_groups(bits)[0])
    sums, pieces, other_own, value_own = lax.optimization_barrier(
        (sums, pieces, other_own, value_own)
    )
    feed_total = last_steps(feed_total, pieces)
    units = after_low.shape[1]
    contract_share = feed_total[:, :units].T
    expand_share = feed_total[:, units:]
    sums = sum_dp(sums, [[0], [1]])
    other_total = first_total(other_own, other_arrived)
    value_total = first_total(value_own, value_arrived)
    other_arrived = send_pieces(other_total, bits_left(0), [1])
    value_arrived = send_pieces(value_total, bits_left(1), [0])
    other_total = add_pieces(other_total, bits_left(0), [1], other_arrived)[0]
    value_total = add_pieces(value_total, bits_left(1), [0], value_arrived)[0]
    mixing_total = last_steps(jnp.concatenate([other_total, value_total], axis=-1), None)
    joined_share = mixing_total[:, : 3 * local].reshape(-1, 3, local)
    output_share = mixing_total[:, 3 * local :].T
    row_sums = sums[: 6 * width].reshape(6, width)
    unit_sums = sums[6 * width :]
    return (
        block_output,
        input_gradient,
        row_sums[0],
        row_sums[1],
        joined_share,
        unit_sums[: 2 * local].reshape(2, local),
        output_share,
        row_sums[2],
        row_sums[3],
        row_sums[4],
        expand_share,
        unit_sums[2 * local :],
        contract_share,
        row_sums[5],
    )


def solution(mesh):
    in_specs = (
        P(("dp", "tensor"), None),
        P("dp"),
        P(),
        P(),
        P(None, None, "tensor"),
        P(None, "tensor"),
        P("tensor", None),
        P(),
        P(),
        P(),
        P(None, "tensor"),
        P("tensor"),
        P("tensor", None),
        P(),
        P(("dp", "tensor"), None),
    )
    out_specs = (
        P(("dp", "tensor"), None),
        P(("dp", "tensor"), None),
        P(),
        P(),
        P("dp", None, "tensor"),
        P(None, "tensor"),
        P("tensor", "dp"),
        P(),
        P(),
        P(),
        P("dp", "tensor"),
        P("tensor"),
        P("tensor", "dp"),
        P(),
    )
    return jax.shard_map(shards, mesh=mesh, in_specs=in_specs, out_specs=out_specs, check_vma=False)
```
